256 devices in a mesh: table: 64 (over z, x, core), replica: 4 (over y).
Axes of the slice: x: 4, y: 4, z: 8, core: 2. Of those that a mesh axis runs over, the one named last changes fastest.
Arguments:
- emb_table: bfloat16 [65536, 128], P('table'), may hold values from -3 to 3
- cross_up: bfloat16 [256, 3456], replicated, may hold values from -0.375 to 0.375
- cross_down: bfloat16 [256, 3456], replicated, may hold values from -0.109375 to 0.109375
- cross_bias: float32 [3456], replicated, may hold values from -3 to 3
- out_weight: float32 [3456], replicated, may hold values from -0.109375 to 0.109375
- bottom_weight: float32 [13, 128], replicated, may hold values from -1.75 to 1.75
- bottom_bias: float32 [128], replicated, may hold values from -3 to 3
- dense_in: float32 [32768, 13], P(('table', 'replica')), may hold values from -6 to 6
- labels: int32 [32768], P(('table', 'replica')), may hold values from 0 to 1
- lookup_ids: int32 [32768, 26, 4], P(('table', 'replica')), may hold values from 0 to 6143
- bag_weight: float32 [32768, 26, 4], P(('table', 'replica')), may hold values from 0.25 to 1
- bag_length: int32 [32768, 26], P(('table', 'replica')), may hold values from 1 to 4
- want_blocks: int32 [64, 4, 64, 1], P('table', 'replica'), may hold values from 0 to 31
- hot_blocks: int32 [64, 2], P('table'), may hold values from 0 to 31
- hot_count: int32 [64], P('table'), may hold values from 1 to 2, as said below
Outputs:
- up_grad: float32 [256, 3456], P(('table', 'replica'))
- down_grad: float32 [256, 3456], P(('table', 'replica'))
- table_grad: float32 [65536, 128], P(('table', 'replica'))
The draws below stay inside these ranges and needn't reach their ends.
Inputs may be any that keep to these rules, and one draw needn't show every extreme that they name: `hot_count`: each owner has 1 to 2 live hot slots, and some owner has 2.
All inputs are finite; a program needn't handle non-finite values.
Results may differ from the reference program's by a relative error of at most 0.0053.
Values may be sent and summed in bfloat16 or wider, within the bound.
No kernel may reach another device: no remote copies, remote signals or barrier semaphores. Data moves between devices by JAX's collectives and lax.ppermute only.
A program may use at most 64 MiB of HBM per device.

```python
import jax
import jax.numpy as jnp
from jax import lax

EMB = 128
FEATS = 26
DENSE = 13
RANK = 256
BLOCK = 32
BAG = 4
WANT = 1
HOT_MOST = 2
B_DEV = 128
BLOCKS_DEV = 32
OWNERS = 64
ROWS = 65536
CACHE = 6144
DI = 3456
SAMPLES = 32768
N_TABLE = 64
N_REPLICA = 4


def draw_hot_count(key, part):
    first_key, second_key = jax.random.split(jax.random.fold_in(key, 7))
    doubled = (jax.random.randint(first_key, (OWNERS,), 0, 4) == 0).astype(jnp.int32) * (HOT_MOST - 1)
    chosen = jax.random.randint(second_key, (), 0, OWNERS)
    return jnp.where(jnp.arange(OWNERS) == chosen, HOT_MOST, 1 + doubled).astype(jnp.int32)


def with_ends(entries, rng, least, high):
    longest = entries.shape.index(max(entries.shape))
    spots = []
    for shift in (0, 1):
        where = [jax.random.randint(jax.random.fold_in(rng, axis), (), 0, length) for axis, length in enumerate(entries.shape)]
        where[longest] = (where[longest] + shift) % entries.shape[longest]
        spots.append(tuple(where))
    return entries.at[spots[0]].set(least).at[spots[1]].set(high)


def shard_levels(own_key, dims, cuts, low, largest):
    gain = 1.0
    for axis_at, shards_of in cuts:
        steps = jax.random.uniform(jax.random.fold_in(jax.random.fold_in(own_key, 6), axis_at), (shards_of,), jnp.float32, low / len(cuts), largest / len(cuts))
        gain = gain * jnp.repeat(jnp.exp(steps), dims[axis_at] // shards_of).reshape((-1,) + (1,) * (len(dims) - 1 - axis_at))
    return gain


def gaussian(rng, shape, scale, bound, pieces=(), kind=jnp.bfloat16):
    result = scale * jax.random.normal(rng, shape, jnp.float32)
    if pieces:
        result = result * shard_levels(rng, shape, pieces, -0.22, 0.18)
    return jnp.clip(result, -bound, bound).astype(kind)


def setup_inputs(seed: int = 0) -> dict:
    streams_of = jax.random.split(jax.random.key(seed), 16)
    return {
        "emb_table": gaussian(streams_of[0], (ROWS, EMB), 0.5, 3.0, ((0, 64),)),
        "cross_up": gaussian(streams_of[1], (RANK, DI), RANK ** -0.5, 0.375),
        "cross_down": gaussian(streams_of[2], (RANK, DI), DI ** -0.5, 0.109375),
        "cross_bias": gaussian(streams_of[3], (DI,), 0.5, 3.0, (), jnp.float32),
        "out_weight": gaussian(streams_of[4], (DI,), DI ** -0.5, 0.109375, (), jnp.float32),
        "bottom_weight": gaussian(streams_of[5], (DENSE, EMB), DENSE ** -0.5, 1.75, (), jnp.float32),
        "bottom_bias": gaussian(streams_of[6], (EMB,), 0.5, 3.0, (), jnp.float32),
        "dense_in": gaussian(streams_of[7], (SAMPLES, DENSE), 1.0, 6.0, ((0, 256),), jnp.float32),
        "labels": with_ends(jax.random.randint(streams_of[8], (SAMPLES,), 0, 2), jax.random.fold_in(streams_of[8], 1), 0, 1).astype(jnp.int32),
        "lookup_ids": with_ends(jax.random.randint(streams_of[9], (SAMPLES, FEATS, BAG), 0, CACHE), jax.random.fold_in(streams_of[9], 1), 0, CACHE - 1).astype(jnp.int32),
        "bag_weight": jnp.clip(0.25 + 0.75 * jax.random.uniform(streams_of[10], (SAMPLES, FEATS, BAG), jnp.float32) ** shard_levels(streams_of[10], (SAMPLES, FEATS, BAG), ((0, 256),), -0.2, 0.2), 0.25, 1.0),
        "bag_length": with_ends(jax.random.randint(streams_of[11], (SAMPLES, FEATS), 1, BAG + 1), jax.random.fold_in(streams_of[11], 1), 1, BAG).astype(jnp.int32),
        "want_blocks": with_ends(jax.random.randint(streams_of[12], (OWNERS, N_REPLICA, OWNERS, WANT), 0, BLOCKS_DEV), jax.random.fold_in(streams_of[12], 1), 0, BLOCKS_DEV - 1).astype(jnp.int32),
        "hot_blocks": with_ends(jax.random.randint(streams_of[13], (OWNERS, HOT_MOST), 0, BLOCKS_DEV), jax.random.fold_in(streams_of[13], 1), 0, BLOCKS_DEV - 1).astype(jnp.int32),
        "hot_count": draw_hot_count(jax.random.fold_in(streams_of[15], 71), 0),
    }


def local_step(cached_rows, dense_dev, labels_dev, ids_dev, weight_dev, length_dev, cross_up, cross_down, cross_bias, out_weight, bottom_weight, bottom_bias):
    batch = ids_dev.shape[0]
    width = cached_rows.shape[1]
    gathered = cached_rows[ids_dev].astype(jnp.float32)
    slots = jnp.arange(ids_dev.shape[2], dtype=jnp.int32)
    bag_coef = jnp.where(slots[None, None, :] < length_dev[:, :, None], weight_dev, jnp.zeros((), jnp.float32))
    pooled = jnp.sum(bag_coef[..., None] * gathered, axis=2)
    bottom = jax.nn.relu(jnp.dot(dense_dev, bottom_weight, precision=lax.Precision.HIGHEST) + bottom_bias)
    cross_base = jnp.concatenate([bottom, pooled.reshape(batch, -1)], 1).astype(jnp.bfloat16)
    low_rank = lax.dot_general(cross_base, cross_down, (((1,), (1,)), ((), ())), preferred_element_type=jnp.float32).astype(jnp.bfloat16)
    cross_gate = jnp.dot(low_rank, cross_up, preferred_element_type=jnp.float32) + cross_bias
    base_wide = cross_base.astype(jnp.float32)
    crossed = base_wide * cross_gate + base_wide
    logits = jnp.dot(crossed, out_weight, precision=lax.Precision.HIGHEST)
    logit_grad = jax.nn.sigmoid(logits) - labels_dev.astype(jnp.float32)
    grad_crossed = logit_grad[:, None] * out_weight[None, :]
    g_cross = (grad_crossed * base_wide).astype(jnp.bfloat16)
    g_low = lax.dot_general(g_cross, cross_up, (((1,), (1,)), ((), ())), preferred_element_type=jnp.float32).astype(jnp.bfloat16)
    up_part = lax.dot_general(low_rank, g_cross, (((0,), (0,)), ((), ())), preferred_element_type=jnp.float32)
    down_part = lax.dot_general(g_low, cross_base, (((0,), (0,)), ((), ())), preferred_element_type=jnp.float32)
    grad_base = grad_crossed * (cross_gate + 1.0) + jnp.dot(g_low, cross_down, preferred_element_type=jnp.float32)
    grad_pooled = grad_base[:, width:].reshape(batch, -1, width)
    contrib = bag_coef[..., None] * grad_pooled[:, :, None, :]
    cache_grad = jnp.zeros(cached_rows.shape, jnp.float32).at[ids_dev.reshape(-1)].add(contrib.reshape(-1, width))
    return up_part, down_part, cache_grad


def reference(emb_table, cross_up, cross_down, cross_bias, out_weight, bottom_weight, bottom_bias, dense_in, labels, lookup_ids, bag_weight, bag_length, want_blocks, hot_blocks, hot_count):
    devices_all = N_TABLE * N_REPLICA
    blocks = emb_table.reshape(OWNERS, BLOCKS_DEV, BLOCK, EMB)
    owner_ids = jnp.arange(OWNERS, dtype=jnp.int32)
    alive = jnp.arange(HOT_MOST, dtype=jnp.int32)[:, None] < hot_count[None, :]
    hot_rows = jnp.where(alive[:, :, None, None], blocks[owner_ids[None, :], hot_blocks.T], jnp.zeros((), jnp.bfloat16))
    hot_flat = hot_rows.reshape(-1, EMB)
    cold_count = OWNERS * WANT * BLOCK
    wanted = want_blocks.reshape(devices_all, OWNERS, WANT)
    items = (wanted,
             dense_in.reshape(devices_all, B_DEV, DENSE),
             labels.reshape(devices_all, B_DEV),
             lookup_ids.reshape(devices_all, B_DEV, FEATS, BAG),
             bag_weight.reshape(devices_all, B_DEV, FEATS, BAG),
             bag_length.reshape(devices_all, B_DEV, FEATS))

    def device_turn(running, device_item):
        block_grad, hot_grad, up_sum, down_sum = running
        wanted_dev, dense_dev, labels_dev, ids_dev, weight_dev, length_dev = device_item
        cold_rows = blocks[owner_ids[:, None], wanted_dev]
        cached_rows = jnp.concatenate([cold_rows.reshape(-1, EMB), hot_flat], 0)
        up_part, down_part, cache_grad = local_step(cached_rows, dense_dev, labels_dev, ids_dev, weight_dev, length_dev, cross_up, cross_down, cross_bias, out_weight, bottom_weight, bottom_bias)
        cold_grad = lax.optimization_barrier(cache_grad[:cold_count].astype(jnp.bfloat16)).astype(jnp.float32)
        block_grad = block_grad.at[owner_ids[:, None], wanted_dev].add(cold_grad.reshape(OWNERS, WANT, BLOCK, EMB))
        hot_grad = hot_grad + cache_grad[cold_count:]
        return (block_grad, hot_grad, up_sum + up_part, down_sum + down_part), None

    start = (jnp.zeros((OWNERS, BLOCKS_DEV, BLOCK, EMB), jnp.float32),
             jnp.zeros((HOT_MOST * OWNERS * BLOCK, EMB), jnp.float32),
             jnp.zeros((RANK, DI), jnp.float32),
             jnp.zeros((RANK, DI), jnp.float32))
    (block_grad, hot_grad, up_sum, down_sum), _ = lax.scan(device_turn, start, items)
    hot_sums = jnp.where(alive[:, :, None, None], hot_grad.reshape(HOT_MOST, OWNERS, BLOCK, EMB), jnp.zeros((), jnp.float32))
    block_grad = block_grad.at[owner_ids[None, :], hot_blocks.T].add(hot_sums)
    return up_sum, down_sum, block_grad.reshape(ROWS, EMB)
```

```python
import functools

import jax
import jax.numpy as jnp
from jax import lax
from jax.experimental import pallas as pl
from jax.experimental.pallas import tpu as pltpu
from jax.sharding import Mesh
from jax.sharding import PartitionSpec as P

EMB = 128
BLOCK = 32
TABLE = ("table_0", "table_1", "table_2")
TABLE_REPLICA = ("table_0", "table_1", "table_2", "replica")
BF = jnp.bfloat16
F32 = jnp.float32


def build_kernel(first, tile, slots_ref, iota_ref, out_ref):
    base = (first + pl.program_id(0) * tile).astype(F32)
    feats, _, batch = slots_ref.shape
    rows = iota_ref[...]

    def one(f, carry):
        packed = slots_ref[f]
        rel = jnp.clip(packed[:4] - base, -1.0, float(tile)).astype(BF)
        coef = packed[4:].astype(BF)
        acc = jnp.zeros((tile, batch), BF)
        for s in range(4):
            hit = rows == jnp.broadcast_to(rel[s : s + 1], (tile, batch))
            acc = jnp.where(hit, jnp.broadcast_to(coef[s : s + 1], (tile, batch)), acc)
        out_ref[:, pl.ds(pl.multiple_of(f * batch, batch), batch)] = acc
        return carry

    lax.fori_loop(0, feats, one, 0)


def build_selection(slots, first, count):
    tile = 256
    feats, _, batch = slots.shape
    bags = feats * batch
    iota = lax.broadcasted_iota(jnp.int32, (tile, batch), 0).astype(BF)
    return pl.pallas_call(
        functools.partial(build_kernel, first, tile),
        grid=(count // tile,),
        in_specs=[
            pl.BlockSpec((feats, 8, batch), lambda i: (0, 0, 0)),
            pl.BlockSpec((tile, batch), lambda i: (0, 0)),
        ],
        out_specs=pl.BlockSpec((tile, bags), lambda i: (i, 0)),
        out_shape=jax.ShapeDtypeStruct((count, bags), BF),
        cost_estimate=pl.CostEstimate(
            flops=count * bags * 8, bytes_accessed=count * bags * 2, transcendentals=0
        ),
        name="build_selection",
    )(slots, iota)


def gather_kernel(rows_ref, sel_ref, out_ref):
    part = lax.dot_general(
        rows_ref[...], sel_ref[...], (((0,), (0,)), ((), ())), preferred_element_type=F32
    )

    @pl.when(pl.program_id(0) == 0)
    def _():
        out_ref[...] = part

    @pl.when(pl.program_id(0) > 0)
    def _():
        out_ref[...] += part


def gather_pooled(rows, sel):
    tile = 512
    count, bags = sel.shape
    return pl.pallas_call(
        gather_kernel,
        grid=(count // tile,),
        in_specs=[
            pl.BlockSpec((tile, EMB), lambda i: (i, 0)),
            pl.BlockSpec((tile, bags), lambda i: (i, 0)),
        ],
        out_specs=pl.BlockSpec((EMB, bags), lambda i: (0, 0)),
        out_shape=jax.ShapeDtypeStruct((EMB, bags), F32),
        cost_estimate=pl.CostEstimate(
            flops=2 * count * bags * EMB, bytes_accessed=count * bags * 2, transcendentals=0
        ),
        name="gather_pooled",
    )(rows, sel)


def cross_kernel(
    rows_ref,
    sel_ref,
    hot_ref,
    scale_ref,
    scale_t_ref,
    bottom_ref,
    labels_ref,
    up_ref,
    down_ref,
    bias_ref,
    ow_ref,
    lines_ref,
    gpool_ref,
    acc,
    base_ref,
):
    step = pl.program_id(0)
    part = lax.dot_general(
        rows_ref[...], sel_ref[...], (((0,), (0,)), ((), ())), preferred_element_type=F32
    )

    @pl.when(step == 0)
    def _():
        acc[...] = hot_ref[...] + part

    @pl.when(step > 0)
    def _():
        acc[...] += part

    @pl.when(step == pl.num_programs(0) - 1)
    def _():
        batch = bottom_ref.shape[0]
        width = up_ref.shape[1]
        feats = width // EMB - 1
        base_ref[:, :EMB] = bottom_ref[...].astype(BF)
        for f in range(feats):
            block = acc[:, f * batch : (f + 1) * batch]
            base_ref[:, (f + 1) * EMB : (f + 2) * EMB] = (block * scale_ref[f : f + 1, :]).T.astype(BF)
        base = base_ref[...]
        nt = (((1,), (1,)), ((), ()))
        tn = (((0,), (0,)), ((), ()))
        low = lax.dot_general(base, down_ref[...], nt, preferred_element_type=F32).astype(BF)
        wide = base.astype(F32)
        ow = ow_ref[...]
        gate = jnp.dot(low, up_ref[...], preferred_element_type=F32) + bias_ref[...]
        crossed = wide * gate + wide
        logits = jnp.sum(crossed * ow, axis=1, keepdims=True)
        lg = jax.nn.sigmoid(logits) - labels_ref[...].astype(F32)
        grad_crossed = lg * ow
        g_cross = (grad_crossed * wide).astype(BF)
        g_low = lax.dot_general(g_cross, up_ref[...], nt, preferred_element_type=F32).astype(BF)
        up_part = lax.dot_general(low, g_cross, tn, preferred_element_type=F32)
        down_part = lax.dot_general(g_low, base, tn, preferred_element_type=F32)
        rank, per = up_part.shape[0], feats + 1
        lines = lines_ref.shape[0] // rank
        for c in range(per):
            lines_ref[pl.ds(c, rank, stride=lines), :] = up_part[:, c * EMB : (c + 1) * EMB]
            lines_ref[pl.ds(per + c, rank, stride=lines), :] = down_part[
                :, c * EMB : (c + 1) * EMB
            ]
        for c in range(2 * per, lines):
            lines_ref[pl.ds(c, rank, stride=lines), :] = jnp.zeros((rank, EMB), F32)
        grad_base = grad_crossed * (gate + 1.0) + jnp.dot(
            g_low, down_ref[...], preferred_element_type=F32
        )
        for f in range(feats):
            block = grad_base[:, (f + 1) * EMB : (f + 2) * EMB] * scale_t_ref[:, f : f + 1]
            gpool_ref[f * batch : (f + 1) * batch, :] = block.astype(BF)


def cross_layer(rows, sel, pooled_hot, scale, bottom, labels, up, down, bias, ow):
    tile = 512
    count, bags = sel.shape
    rank, width = up.shape
    batch = bottom.shape[0]
    lines = rank * pl.cdiv(2 * width // EMB, 8) * 8
    whole = lambda *shape: pl.BlockSpec(shape, lambda i: (0,) * len(shape))
    return pl.pallas_call(
        cross_kernel,
        grid=(count // tile,),
        in_specs=[
            pl.BlockSpec((tile, EMB), lambda i: (i, 0)),
            pl.BlockSpec((tile, bags), lambda i: (i, 0)),
            whole(EMB, bags),
            whole(*scale.shape),
            whole(batch, scale.shape[0]),
            whole(batch, EMB),
            whole(batch, 1),
            whole(rank, width),
            whole(rank, width),
            whole(1, width),
            whole(1, width),
        ],
        out_specs=[whole(lines, EMB), whole(bags, EMB)],
        out_shape=[
            jax.ShapeDtypeStruct((lines, EMB), F32),
            jax.ShapeDtypeStruct((bags, EMB), BF),
        ],
        scratch_shapes=[
            pltpu.VMEM((EMB, bags), F32),
            pltpu.VMEM((batch, width), BF),
        ],
        cost_estimate=pl.CostEstimate(
            flops=2 * count * bags * EMB + 12 * batch * rank * width,
            bytes_accessed=count * bags * 2 + 8 * rank * width,
            transcendentals=batch,
        ),
        name="cross_layer",
    )(rows, sel, pooled_hot, scale, scale.T, bottom, labels, up, down, bias, ow)


def scatter_kernel(sel_ref, grad_ref, out_ref):
    out_ref[...] = jnp.dot(
        sel_ref[...], grad_ref[...], preferred_element_type=F32
    ).astype(out_ref.dtype)


def scatter_rows(sel, grad, dtype):
    tile = 512
    count, bags = sel.shape
    return pl.pallas_call(
        scatter_kernel,
        grid=(count // tile,),
        in_specs=[
            pl.BlockSpec((tile, bags), lambda i: (i, 0)),
            pl.BlockSpec((bags, EMB), lambda i: (0, 0)),
        ],
        out_specs=pl.BlockSpec((tile, EMB), lambda i: (i, 0)),
        out_shape=jax.ShapeDtypeStruct((count, EMB), dtype),
        cost_estimate=pl.CostEstimate(
            flops=2 * count * bags * EMB, bytes_accessed=count * bags * 2, transcendentals=0
        ),
        name="scatter_rows",
    )(sel, grad)


def hot_kernel(count_ref, picks_ref, block_ref, out_ref):
    live = pl.program_id(0) < count_ref[0]
    rows = block_ref[...]
    out_ref[...] = jnp.where(live, rows, jnp.zeros_like(rows))


def own_hot_rows(emb_table, picks, count):
    slots = picks.shape[0]
    return pl.pallas_call(
        hot_kernel,
        grid_spec=pltpu.PrefetchScalarGridSpec(
            num_scalar_prefetch=2,
            grid=(slots,),
            in_specs=[pl.BlockSpec((BLOCK, EMB), lambda s, count, picks: (picks[s], 0))],
            out_specs=pl.BlockSpec((BLOCK, EMB), lambda s, count, picks: (s, 0)),
        ),
        out_shape=jax.ShapeDtypeStruct((slots * BLOCK, EMB), BF),
        name="own_hot_rows",
    )(count, picks, emb_table)


def serve_kernel(picks_ref, table_ref, out_ref):
    for i in range(out_ref.shape[0]):
        start = pl.multiple_of(picks_ref[i] * BLOCK, BLOCK)
        out_ref[i] = table_ref[pl.ds(start, BLOCK), :]


def served_blocks(emb_table, picks):
    owners = picks.shape[0]
    return pl.pallas_call(
        serve_kernel,
        in_specs=[
            pl.BlockSpec(memory_space=pltpu.SMEM),
            pl.BlockSpec(memory_space=pltpu.VMEM),
        ],
        out_shape=jax.ShapeDtypeStruct((owners, BLOCK, EMB), BF),
        name="served_blocks",
    )(picks, emb_table)


def collect_kernel(picks_ref, hot_picks_ref, count_ref, back_ref, hot_ref, out_ref, acc):
    acc[...] = jnp.zeros_like(acc)
    for i in range(back_ref.shape[0]):
        start = pl.multiple_of(picks_ref[i] * BLOCK, BLOCK)
        acc[pl.ds(start, BLOCK), :] += back_ref[i].astype(F32)
    for s in range(hot_picks_ref.shape[0]):
        start = pl.multiple_of(hot_picks_ref[s] * BLOCK, BLOCK)
        hot = hot_ref[s * BLOCK : (s + 1) * BLOCK, :]
        acc[pl.ds(start, BLOCK), :] += jnp.where(s < count_ref[0], hot, jnp.zeros_like(hot))
    out_ref[...] = acc[...].astype(out_ref.dtype)


def collected(rows, picks, hot_picks, count, back, hot):
    smem = pl.BlockSpec(memory_space=pltpu.SMEM)
    vmem = pl.BlockSpec(memory_space=pltpu.VMEM)
    return pl.pallas_call(
        collect_kernel,
        in_specs=[smem, smem, smem, vmem, vmem],
        out_shape=jax.ShapeDtypeStruct((rows, EMB), BF),
        scratch_shapes=[pltpu.VMEM((rows, EMB), F32)],
        name="collected",
    )(picks, hot_picks, count, back, hot)


def slots_kernel(cold, hot_slots, tries, ids_ref, weight_ref, length_ref, slots_ref, scale_ref):
    bag = ids_ref.shape[0]
    length = length_ref[...]
    row_bits = BLOCK.bit_length() - 1
    cold_bits = cold.bit_length() - 1
    ids, coef = [], []
    for s in range(bag):
        i = ids_ref[s]
        h = i - cold
        slot, rest = h >> cold_bits, h & (cold - 1)
        moved = cold + ((rest >> row_bits) * hot_slots + slot) * BLOCK + (rest & (BLOCK - 1))
        ids.append(jnp.where(i < cold, i, moved))
        coef.append(jnp.where(s < length, weight_ref[s], 0.0))
    total = []
    for j in range(bag):
        c = coef[j]
        for i in range(j):
            c = c + jnp.where(ids[i] == ids[j], coef[i], 0.0)
        total.append(c)
    kept = []
    for j in range(bag):
        c = total[j]
        for k in range(j + 1, bag):
            c = jnp.where(ids[j] == ids[k], 0.0, c)
        kept.append(c)
    largest = functools.reduce(jnp.maximum, kept)
    inverse = 1.0 / largest

    def attempt(k, carry):
        best, scale, factor = carry
        t = 1.0 + k.astype(F32) * (1.0 / tries)
        up = inverse * t
        back = largest * (1.0 / t)
        err = jnp.zeros_like(largest)
        for c in kept:
            miss = (c * up).astype(BF).astype(F32) * back - c
            err = err + miss * miss
        better = err < best
        return (
            jnp.where(better, err, best),
            jnp.where(better, back, scale),
            jnp.where(better, up, factor),
        )

    start = (jnp.full_like(largest, jnp.inf), largest, inverse)
    _, scale, factor = lax.fori_loop(0, tries, attempt, start)
    for s in range(bag):
        slots_ref[s] = ids[s].astype(F32)
        slots_ref[bag + s] = kept[s] * factor
    scale_ref[...] = scale


def bag_slots(ids, weight, length, owners, hot_slots):
    cold = owners * BLOCK
    batch, feats, bag = ids.shape
    slots, scale = pl.pallas_call(
        functools.partial(slots_kernel, cold, hot_slots, 64),
        out_shape=[
            jax.ShapeDtypeStruct((2 * bag, feats, batch), F32),
            jax.ShapeDtypeStruct((feats, batch), F32),
        ],
        name="bag_slots",
    )(jnp.transpose(ids, (2, 1, 0)), jnp.transpose(weight, (2, 1, 0)), length.T)
    return jnp.transpose(slots, (1, 0, 2)), scale


def local(
    emb_table,
    cross_up,
    cross_down,
    cross_bias,
    out_weight,
    bottom_weight,
    bottom_bias,
    dense_in,
    labels,
    lookup_ids,
    bag_weight,
    bag_length,
    want_blocks,
    hot_blocks,
    hot_count,
):
    owners = lax.axis_size(TABLE)
    replicas = lax.axis_size("replica")
    hot_slots = hot_blocks.shape[1]
    _, width = cross_up.shape

    own_hot = own_hot_rows(emb_table, hot_blocks[0], hot_count)
    hot_rows = lax.all_gather(own_hot, TABLE, axis=0, tiled=True)

    wanted = want_blocks.reshape(owners, 1, 1)
    asked_for = lax.all_to_all(wanted, TABLE, split_axis=0, concat_axis=0, tiled=True)
    asked_for = asked_for.reshape(owners)
    served = served_blocks(emb_table, asked_for)
    cold_rows = lax.all_to_all(served, TABLE, split_axis=0, concat_axis=0, tiled=True)
    cold_rows = cold_rows.reshape(-1, EMB)
    cold_count = cold_rows.shape[0]
    hot_total = hot_rows.shape[0]

    slots, scale = bag_slots(lookup_ids, bag_weight, bag_length, owners, hot_slots)
    sel_cold = build_selection(slots, 0, cold_count)
    sel_hot = build_selection(slots, cold_count, hot_total)

    bottom = jax.nn.relu(
        jnp.dot(dense_in, bottom_weight, precision=lax.Precision.HIGHEST) + bottom_bias
    )
    pooled_hot = gather_pooled(hot_rows, sel_hot)
    grads, grad_pooled = cross_layer(
        cold_rows,
        sel_cold,
        pooled_hot,
        scale,
        bottom,
        labels[:, None],
        cross_up,
        cross_down,
        cross_bias[None],
        out_weight[None],
    )

    weights = lax.psum_scatter(grads, TABLE, scatter_dimension=0, tiled=True)

    hot_grad = scatter_rows(sel_hot, grad_pooled, F32)
    hot_mine = lax.psum_scatter(hot_grad, TABLE, scatter_dimension=0, tiled=True)
    cold_grad = scatter_rows(sel_cold, grad_pooled, BF).reshape(owners, BLOCK, EMB)
    returned = lax.all_to_all(cold_grad, TABLE, split_axis=0, concat_axis=0, tiled=True)
    block_grad = collected(
        emb_table.shape[0], asked_for, hot_blocks[0], hot_count, returned, hot_mine
    )

    block_part = block_grad.reshape(replicas, -1, EMB)
    weight_part = weights.astype(BF).reshape(replicas, -1, EMB)
    both = jnp.concatenate([block_part, weight_part], 1)
    both = lax.all_to_all(both, "replica", split_axis=0, concat_axis=0, tiled=True)
    both = both.astype(F32).sum(axis=0)
    table_grad = both[: block_part.shape[1]]
    per = 2 * width // EMB
    mine = both[block_part.shape[1] :][:per].reshape(1, 2 * width)
    up_grad, down_grad = mine[:, :width], mine[:, width:]
    return (up_grad, down_grad, table_grad)


def solution(mesh):
    torus = Mesh(
        mesh.devices.reshape(8, 4, 2, mesh.shape["replica"]),
        ("table_0", "table_1", "table_2", "replica"),
    )
    in_specs = (
        P(TABLE, None),
        P(),
        P(),
        P(),
        P(),
        P(),
        P(),
        P(TABLE_REPLICA, None),
        P(TABLE_REPLICA),
        P(TABLE_REPLICA, None, None),
        P(TABLE_REPLICA, None, None),
        P(TABLE_REPLICA, None),
        P(TABLE, "replica", None, None),
        P(TABLE, None),
        P(TABLE),
    )
    out_specs = (P(TABLE_REPLICA, None), P(TABLE_REPLICA, None), P(TABLE_REPLICA, None))
    return jax.shard_map(local, mesh=torus, in_specs=in_specs, out_specs=out_specs, check_vma=False)
```

```python
import functools

import jax
import jax.numpy as jnp
from jax import lax
from jax.experimental import pallas as pl
from jax.experimental.pallas import tpu as pltpu
from jax.sharding import Mesh
from jax.sharding import PartitionSpec as P

EMB = 128
BLOCK = 32
TABLE = ("table_0", "table_1", "table_2")
FAR = "table_0"
NEAR = ("table_1", "table_2", "replica")
TABLE_REPLICA = ("table_0", "table_1", "table_2", "replica")
BF = jnp.bfloat16
F32 = jnp.float32


def build_kernel(first, tile, slots_ref, iota_ref, out_ref):
    base = (first + pl.program_id(0) * tile).astype(F32)
    feats, _, batch = slots_ref.shape
    rows = iota_ref[...]

    def one(f, carry):
        packed = slots_ref[f]
        rel = jnp.clip(packed[:4] - base, -1.0, float(tile)).astype(BF)
        coef = packed[4:].astype(BF)
        acc = jnp.zeros((tile, batch), BF)
        for s in range(4):
            hit = rows == jnp.broadcast_to(rel[s : s + 1], (tile, batch))
            acc = jnp.where(hit, jnp.broadcast_to(coef[s : s + 1], (tile, batch)), acc)
        out_ref[:, pl.ds(pl.multiple_of(f * batch, batch), batch)] = acc
        return carry

    lax.fori_loop(0, feats, one, 0)


def build_selection(slots, first, count):
    tile = 256
    feats, _, batch = slots.shape
    bags = feats * batch
    iota = lax.broadcasted_iota(jnp.int32, (tile, batch), 0).astype(BF)
    return pl.pallas_call(
        functools.partial(build_kernel, first, tile),
        grid=(count // tile,),
        in_specs=[
            pl.BlockSpec((feats, 8, batch), lambda i: (0, 0, 0)),
            pl.BlockSpec((tile, batch), lambda i: (0, 0)),
        ],
        out_specs=pl.BlockSpec((tile, bags), lambda i: (i, 0)),
        out_shape=jax.ShapeDtypeStruct((count, bags), BF),
        cost_estimate=pl.CostEstimate(
            flops=count * bags * 8, bytes_accessed=count * bags * 2, transcendentals=0
        ),
        name="build_selection",
    )(slots, iota)


def cross_kernel(
    near,
    rows_ref,
    sel_ref,
    scale_ref,
    scale_t_ref,
    bottom_ref,
    labels_ref,
    up_ref,
    down_ref,
    bias_ref,
    ow_ref,
    grads_ref,
    gpool_ref,
    acc,
    base_ref,
    lines_ref,
):
    step = pl.program_id(0)
    part = lax.dot_general(
        rows_ref[...], sel_ref[...], (((0,), (0,)), ((), ())), preferred_element_type=F32
    )

    @pl.when(step == 0)
    def _():
        acc[...] = part

    @pl.when(step > 0)
    def _():
        acc[...] += part

    @pl.when(step == pl.num_programs(0) - 1)
    def _():
        batch = bottom_ref.shape[0]
        width = up_ref.shape[1]
        feats = width // EMB - 1
        base_ref[:, :EMB] = bottom_ref[...].astype(BF)
        for f in range(feats):
            block = acc[:, f * batch : (f + 1) * batch]
            base_ref[:, (f + 1) * EMB : (f + 2) * EMB] = (block * scale_ref[f : f + 1, :]).T.astype(BF)
        base = base_ref[...]
        nt = (((1,), (1,)), ((), ()))
        tn = (((0,), (0,)), ((), ()))
        low = lax.dot_general(base, down_ref[...], nt, preferred_element_type=F32).astype(BF)
        wide = base.astype(F32)
        ow = ow_ref[...]
        gate = jnp.dot(low, up_ref[...], preferred_element_type=F32) + bias_ref[...]
        crossed = wide * gate + wide
        logits = jnp.sum(crossed * ow, axis=1, keepdims=True)
        lg = jax.nn.sigmoid(logits) - labels_ref[...].astype(F32)
        grad_crossed = lg * ow
        g_cross = (grad_crossed * wide).astype(BF)
        g_low = lax.dot_general(g_cross, up_ref[...], nt, preferred_element_type=F32).astype(BF)
        up_part = lax.dot_general(low, g_cross, tn, preferred_element_type=F32)
        down_part = lax.dot_general(g_low, base, tn, preferred_element_type=F32)
        rank, per = up_part.shape[0], feats + 1
        lines = lines_ref.shape[0] // rank
        far = rank // near
        for z in range(far):
            part_rows = slice(z * near, (z + 1) * near)
            for c in range(lines):
                if c < per:
                    part = up_part[part_rows, c * EMB : (c + 1) * EMB]
                elif c < 2 * per:
                    part = down_part[part_rows, (c - per) * EMB : (c - per + 1) * EMB]
                else:
                    part = jnp.zeros((near, EMB), F32)
                lines_ref[pl.ds(z * lines + c, near, stride=far * lines), :] = part
        grads_ref[...] = lines_ref[...].astype(BF)
        grad_base = grad_crossed * (gate + 1.0) + jnp.dot(
            g_low, down_ref[...], preferred_element_type=F32
        )
        for f in range(feats):
            block = grad_base[:, (f + 1) * EMB : (f + 2) * EMB] * scale_t_ref[:, f : f + 1]
            gpool_ref[f * batch : (f + 1) * batch, :] = block.astype(BF)


def cross_layer(near, rows, sel, scale, bottom, labels, up, down, bias, ow):
    tile = 512
    count, bags = sel.shape
    rank, width = up.shape
    batch = bottom.shape[0]
    lines = rank * pl.cdiv(2 * width // EMB, 8) * 8
    whole = lambda *shape: pl.BlockSpec(shape, lambda i: (0,) * len(shape))
    return pl.pallas_call(
        functools.partial(cross_kernel, near),
        grid=(count // tile,),
        in_specs=[
            pl.BlockSpec((tile, EMB), lambda i: (i, 0)),
            pl.BlockSpec((tile, bags), lambda i: (i, 0)),
            whole(*scale.shape),
            whole(batch, scale.shape[0]),
            whole(batch, EMB),
            whole(batch, 1),
            whole(rank, width),
            whole(rank, width),
            whole(1, width),
            whole(1, width),
        ],
        out_specs=[whole(lines, EMB), whole(bags, EMB)],
        out_shape=[
            jax.ShapeDtypeStruct((lines, EMB), BF),
            jax.ShapeDtypeStruct((bags, EMB), BF),
        ],
        scratch_shapes=[
            pltpu.VMEM((EMB, bags), F32),
            pltpu.VMEM((batch, width), BF),
            pltpu.VMEM((lines, EMB), F32),
        ],
        cost_estimate=pl.CostEstimate(
            flops=2 * count * bags * EMB + 12 * batch * rank * width,
            bytes_accessed=count * bags * 2 + 8 * rank * width,
            transcendentals=batch,
        ),
        name="cross_layer",
    )(rows, sel, scale, scale.T, bottom, labels, up, down, bias, ow)


def scatter_kernel(sel_ref, grad_ref, out_ref):
    out_ref[...] = jnp.dot(
        sel_ref[...], grad_ref[...], preferred_element_type=F32
    ).astype(out_ref.dtype)


def scatter_rows(sel, grad, dtype):
    tile = 512
    count, bags = sel.shape
    return pl.pallas_call(
        scatter_kernel,
        grid=(count // tile,),
        in_specs=[
            pl.BlockSpec((tile, bags), lambda i: (i, 0)),
            pl.BlockSpec((bags, EMB), lambda i: (0, 0)),
        ],
        out_specs=pl.BlockSpec((tile, EMB), lambda i: (i, 0)),
        out_shape=jax.ShapeDtypeStruct((count, EMB), dtype),
        cost_estimate=pl.CostEstimate(
            flops=2 * count * bags * EMB, bytes_accessed=count * bags * 2, transcendentals=0
        ),
        name="scatter_rows",
    )(sel, grad)


def serve_kernel(picks_ref, hot_picks_ref, count_ref, table_ref, out_ref):
    hot = []
    for s in range(hot_picks_ref.shape[0]):
        start = pl.multiple_of(hot_picks_ref[s] * BLOCK, BLOCK)
        rows = table_ref[pl.ds(start, BLOCK), :]
        hot.append(jnp.where(s < count_ref[0], rows, jnp.zeros_like(rows)))
    for i in range(out_ref.shape[0]):
        start = pl.multiple_of(picks_ref[i] * BLOCK, BLOCK)
        out_ref[i, :BLOCK, :] = table_ref[pl.ds(start, BLOCK), :]
        for s, rows in enumerate(hot):
            out_ref[i, (s + 1) * BLOCK : (s + 2) * BLOCK, :] = rows


def served_rows(emb_table, picks, hot_picks, count):
    smem = pl.BlockSpec(memory_space=pltpu.SMEM)
    vmem = pl.BlockSpec(memory_space=pltpu.VMEM)
    share = (1 + hot_picks.shape[0]) * BLOCK
    return pl.pallas_call(
        serve_kernel,
        in_specs=[smem, smem, smem, vmem],
        out_shape=jax.ShapeDtypeStruct((picks.shape[0], share, EMB), BF),
        name="served_rows",
    )(picks, hot_picks, count, emb_table)


def collect_kernel(picks_ref, hot_picks_ref, count_ref, me_ref, back_ref, own_ref, *others):
    *send_refs, acc = others
    acc[...] = jnp.zeros_like(acc)
    peers, share, _ = back_ref.shape
    hot = jnp.zeros((share - BLOCK, EMB), F32)
    for i in range(peers):
        start = pl.multiple_of(picks_ref[i] * BLOCK, BLOCK)
        acc[pl.ds(start, BLOCK), :] += back_ref[i, :BLOCK, :].astype(F32)
        hot = hot + back_ref[i, BLOCK:, :].astype(F32)
    for s in range(hot_picks_ref.shape[0]):
        start = pl.multiple_of(hot_picks_ref[s] * BLOCK, BLOCK)
        rows = hot[s * BLOCK : (s + 1) * BLOCK]
        acc[pl.ds(start, BLOCK), :] += jnp.where(s < count_ref[0], rows, jnp.zeros_like(rows))
    part, parts = own_ref.shape[0], len(send_refs) + 1
    for k, ref in enumerate((own_ref, *send_refs)):
        whose = lax.rem(me_ref[0] + k, parts)
        start = pl.multiple_of(whose * part, part)
        ref[...] = acc[pl.ds(start, part), :].astype(ref.dtype)


def collected(rows, parts, picks, hot_picks, count, me, back):
    smem = pl.BlockSpec(memory_space=pltpu.SMEM)
    vmem = pl.BlockSpec(memory_space=pltpu.VMEM)
    return pl.pallas_call(
        collect_kernel,
        in_specs=[smem, smem, smem, smem, vmem],
        out_shape=[
            jax.ShapeDtypeStruct((rows // parts, EMB), BF if k else F32) for k in range(parts)
        ],
        scratch_shapes=[pltpu.VMEM((rows, EMB), F32)],
        name="collected",
    )(picks, hot_picks, count, me, back)


def slots_kernel(cold, hot_slots, tries, ids_ref, weight_ref, length_ref, slots_ref, scale_ref):
    bag = ids_ref.shape[0]
    length = length_ref[...]
    row_bits = BLOCK.bit_length() - 1
    cold_bits = cold.bit_length() - 1
    ids, coef = [], []
    for s in range(bag):
        i = ids_ref[s]
        slot, rest = i >> cold_bits, i & (cold - 1)
        owner, row = rest >> row_bits, rest & (BLOCK - 1)
        ids.append((owner * (1 + hot_slots) + slot) * BLOCK + row)
        coef.append(jnp.where(s < length, weight_ref[s], 0.0))
    total = []
    for j in range(bag):
        c = coef[j]
        for i in range(j):
            c = c + jnp.where(ids[i] == ids[j], coef[i], 0.0)
        total.append(c)
    kept = []
    for j in range(bag):
        c = total[j]
        for k in range(j + 1, bag):
            c = jnp.where(ids[j] == ids[k], 0.0, c)
        kept.append(c)
    largest = functools.reduce(jnp.maximum, kept)
    inverse = 1.0 / largest

    def attempt(k, carry):
        best, scale, factor = carry
        t = 1.0 + k.astype(F32) * (1.0 / tries)
        up = inverse * t
        back = largest * (1.0 / t)
        err = jnp.zeros_like(largest)
        for c in kept:
            miss = (c * up).astype(BF).astype(F32) * back - c
            err = err + miss * miss
        better = err < best
        return (
            jnp.where(better, err, best),
            jnp.where(better, back, scale),
            jnp.where(better, up, factor),
        )

    start = (jnp.full_like(largest, jnp.inf), largest, inverse)
    _, scale, factor = lax.fori_loop(0, tries, attempt, start)
    for s in range(bag):
        slots_ref[s] = ids[s].astype(F32)
        slots_ref[bag + s] = kept[s] * factor
    scale_ref[...] = scale


def bag_slots(ids, weight, length, owners, hot_slots):
    cold = owners * BLOCK
    batch, feats, bag = ids.shape
    slots, scale = pl.pallas_call(
        functools.partial(slots_kernel, cold, hot_slots, 64),
        out_shape=[
            jax.ShapeDtypeStruct((2 * bag, feats, batch), F32),
            jax.ShapeDtypeStruct((feats, batch), F32),
        ],
        name="bag_slots",
    )(jnp.transpose(ids, (2, 1, 0)), jnp.transpose(weight, (2, 1, 0)), length.T)
    return jnp.transpose(slots, (1, 0, 2)), scale


def local(
    emb_table,
    cross_up,
    cross_down,
    cross_bias,
    out_weight,
    bottom_weight,
    bottom_bias,
    dense_in,
    labels,
    lookup_ids,
    bag_weight,
    bag_length,
    want_blocks,
    hot_blocks,
    hot_count,
):
    owners = lax.axis_size(TABLE)
    replicas = lax.axis_size("replica")
    hot_slots = hot_blocks.shape[1]
    rank, width = cross_up.shape

    wanted = want_blocks.reshape(owners, 1, 1)
    asked_for = lax.all_to_all(wanted, TABLE, split_axis=0, concat_axis=0, tiled=True)
    asked_for = asked_for.reshape(owners)
    served = served_rows(emb_table, asked_for, hot_blocks[0], hot_count)
    fetched = lax.all_to_all(served, TABLE, split_axis=0, concat_axis=0, tiled=True)
    shares = fetched.shape
    fetched = fetched.reshape(-1, EMB)

    slots, scale = bag_slots(lookup_ids, bag_weight, bag_length, owners, hot_slots)
    sel = build_selection(slots, 0, fetched.shape[0])

    bottom = jax.nn.relu(
        jnp.dot(dense_in, bottom_weight, precision=lax.Precision.HIGHEST) + bottom_bias
    )
    far = lax.axis_size(FAR)
    near = lax.axis_size(NEAR)
    grads, grad_pooled = cross_layer(
        near,
        fetched,
        sel,
        scale,
        bottom,
        labels[:, None],
        cross_up,
        cross_down,
        cross_bias[None],
        out_weight[None],
    )

    parts = lax.all_to_all(
        grads.reshape(near, -1, EMB), NEAR, split_axis=0, concat_axis=0, tiled=True
    )

    row_grad = scatter_rows(sel, grad_pooled, BF).reshape(shares)
    row_grad, parts = lax.optimization_barrier((row_grad, parts))
    returned = lax.all_to_all(row_grad, TABLE, split_axis=0, concat_axis=0, tiled=True)
    nearer = parts.astype(F32).sum(axis=0).astype(BF).reshape(far, -1, EMB)
    nearer, returned = lax.optimization_barrier((nearer, returned))
    own, *sends = collected(
        emb_table.shape[0],
        replicas,
        asked_for,
        hot_blocks[0],
        hot_count,
        lax.axis_index("replica").reshape(1),
        returned,
    )
    table_grad = own
    for k, part in enumerate(sends, 1):
        ring = [(i, (i + k) % replicas) for i in range(replicas)]
        table_grad = table_grad + lax.ppermute(part, "replica", ring).astype(F32)

    mine = lax.all_to_all(nearer, FAR, split_axis=0, concat_axis=0, tiled=True)
    per = 2 * width // EMB
    mine = mine.astype(F32).sum(axis=0)[:per].reshape(rank // (near * far), 2 * width)
    up_grad, down_grad = mine[:, :width], mine[:, width:]
    return (up_grad, down_grad, table_grad)


def solution(mesh):
    torus = Mesh(
        mesh.devices.reshape(8, 4, 2, mesh.shape["replica"]),
        ("table_0", "table_1", "table_2", "replica"),
    )
    in_specs = (
        P(TABLE, None),
        P(),
        P(),
        P(),
        P(),
        P(),
        P(),
        P(TABLE_REPLICA, None),
        P(TABLE_REPLICA),
        P(TABLE_REPLICA, None, None),
        P(TABLE_REPLICA, None, None),
        P(TABLE_REPLICA, None),
        P(TABLE, "replica", None, None),
        P(TABLE, None),
        P(TABLE),
    )
    out_specs = (P(TABLE_REPLICA, None), P(TABLE_REPLICA, None), P(TABLE_REPLICA, None))
    return jax.shard_map(local, mesh=torus, in_specs=in_specs, out_specs=out_specs, check_vma=False)
```

```python
import functools

import jax
import jax.numpy as jnp
from jax import lax
from jax.experimental import pallas as pl
from jax.experimental.pallas import tpu as pltpu
from jax.sharding import Mesh
from jax.sharding import PartitionSpec as P

EMB = 128
BLOCK = 32
TABLE = ("table_0", "table_1", "table_2")
TABLE_REPLICA = ("table_0", "table_1", "table_2", "replica")
BF = jnp.bfloat16
F32 = jnp.float32
XS = 4


def build_kernel(first, tile, slots_ref, out_ref):
    base = (first + pl.program_id(0) * tile).astype(F32)
    feats, _, batch = slots_ref.shape
    rows = lax.broadcasted_iota(jnp.int32, (tile, batch), 0).astype(F32).astype(BF)

    def one(f, carry):
        packed = slots_ref[f]
        rel = jnp.clip(packed[:4] - base, -1.0, float(tile)).astype(BF)
        coef = packed[4:].astype(BF)
        acc = jnp.zeros((tile, batch), BF)
        for s in range(4):
            hit = rows == jnp.broadcast_to(rel[s : s + 1], (tile, batch))
            acc = jnp.where(hit, jnp.broadcast_to(coef[s : s + 1], (tile, batch)), acc)
        out_ref[:, pl.ds(pl.multiple_of(f * batch, batch), batch)] = acc
        return carry

    lax.fori_loop(0, feats, one, 0)


def build_selection(slots, first, count):
    tile = 256
    feats, _, batch = slots.shape
    bags = feats * batch
    return pl.pallas_call(
        functools.partial(build_kernel, first, tile),
        grid=(count // tile,),
        in_specs=[
            pl.BlockSpec((feats, 8, batch), lambda i: (0, 0, 0)),
        ],
        out_specs=pl.BlockSpec((tile, bags), lambda i: (i, 0)),
        out_shape=jax.ShapeDtypeStruct((count, bags), BF),
        cost_estimate=pl.CostEstimate(
            flops=count * bags * 8, bytes_accessed=count * bags * 2, transcendentals=0
        ),
        name="build_selection",
    )(slots)


def cross_kernel(
    near,
    replicas,
    me_ref,
    rows_ref,
    sel_ref,
    scale_ref,
    scale_t_ref,
    bottom_ref,
    labels_ref,
    up_ref,
    down_ref,
    bias_ref,
    ow_ref,
    gpool_ref,
    own_ref,
    *others,
):
    *send_refs, acc, base_ref, lines_ref = others
    step = pl.program_id(0)
    part = lax.dot_general(
        rows_ref[...], sel_ref[...], (((0,), (0,)), ((), ())), preferred_element_type=F32
    )

    @pl.when(step == 0)
    def _():
        acc[...] = part

    @pl.when(step > 0)
    def _():
        acc[...] += part

    @pl.when(step == pl.num_programs(0) - 1)
    def _():
        batch = bottom_ref.shape[0]
        width = up_ref.shape[1]
        feats = width // EMB - 1
        base_ref[:, :EMB] = bottom_ref[...].astype(BF)
        for f in range(feats):
            block = acc[:, f * batch : (f + 1) * batch]
            base_ref[:, (f + 1) * EMB : (f + 2) * EMB] = (block * scale_ref[f : f + 1, :]).T.astype(BF)
        base = base_ref[...]
        nt = (((1,), (1,)), ((), ()))
        tn = (((0,), (0,)), ((), ()))
        low = lax.dot_general(base, down_ref[...], nt, preferred_element_type=F32).astype(BF)
        wide = base.astype(F32)
        ow = ow_ref[...]
        gate = jnp.dot(low, up_ref[...], preferred_element_type=F32) + bias_ref[...]
        crossed = wide * gate + wide
        logits = jnp.sum(crossed * ow, axis=1, keepdims=True)
        lg = jax.nn.sigmoid(logits) - labels_ref[...].astype(F32)
        grad_crossed = lg * ow
        g_cross = (grad_crossed * wide).astype(BF)
        g_low = lax.dot_general(g_cross, up_ref[...], nt, preferred_element_type=F32).astype(BF)
        up_part = lax.dot_general(low, g_cross, tn, preferred_element_type=F32)
        down_part = lax.dot_general(g_low, base, tn, preferred_element_type=F32)
        rank, per = up_part.shape[0], feats + 1
        lines = lines_ref.shape[0] // rank
        far = rank // near
        for z in range(far):
            part_rows = slice(z * near, (z + 1) * near)
            for c in range(lines):
                if c < per:
                    part = up_part[part_rows, c * EMB : (c + 1) * EMB]
                elif c < 2 * per:
                    part = down_part[part_rows, (c - per) * EMB : (c - per + 1) * EMB]
                else:
                    part = jnp.zeros((near, EMB), F32)
                place = (z % XS) * (far // XS) + z // XS
                lines_ref[pl.ds(place * lines + c, near, stride=far * lines), :] = part
        for k, ref in enumerate((own_ref, *send_refs)):
            whose = lax.rem(me_ref[0] + k, replicas)
            for core in range(near // replicas):
                start = pl.multiple_of((core * replicas + whose) * far * lines, far * lines)
                ref[core] = lines_ref[pl.ds(start, far * lines), :].astype(ref.dtype)
        grad_base = grad_crossed * (gate + 1.0) + jnp.dot(
            g_low, down_ref[...], preferred_element_type=F32
        )
        for f in range(feats):
            block = grad_base[:, (f + 1) * EMB : (f + 2) * EMB] * scale_t_ref[:, f : f + 1]
            gpool_ref[f * batch : (f + 1) * batch, :] = block.astype(BF)


def cross_layer(near, replicas, me, rows, sel, scale, bottom, labels, up, down, bias, ow):
    tile = 512
    count, bags = sel.shape
    rank, width = up.shape
    batch = bottom.shape[0]
    lines = rank * pl.cdiv(2 * width // EMB, 8) * 8
    part = (near // replicas, lines // near, EMB)
    whole = lambda *shape: pl.BlockSpec(shape, lambda i: (0,) * len(shape))
    return pl.pallas_call(
        functools.partial(cross_kernel, near, replicas),
        grid=(count // tile,),
        in_specs=[
            pl.BlockSpec(memory_space=pltpu.SMEM),
            pl.BlockSpec((tile, EMB), lambda i: (i, 0)),
            pl.BlockSpec((tile, bags), lambda i: (i, 0)),
            whole(*scale.shape),
            whole(batch, scale.shape[0]),
            whole(batch, EMB),
            whole(batch, 1),
            whole(rank, width),
            whole(rank, width),
            whole(1, width),
            whole(1, width),
        ],
        out_specs=[whole(bags, EMB)] + [whole(*part)] * replicas,
        out_shape=[
            jax.ShapeDtypeStruct((bags, EMB), BF),
            *(jax.ShapeDtypeStruct(part, BF if k else F32) for k in range(replicas)),
        ],
        scratch_shapes=[
            pltpu.VMEM((EMB, bags), F32),
            pltpu.VMEM((batch, width), BF),
            pltpu.VMEM((lines, EMB), F32),
        ],
        cost_estimate=pl.CostEstimate(
            flops=2 * count * bags * EMB + 12 * batch * rank * width,
            bytes_accessed=count * bags * 2 + 8 * rank * width,
            transcendentals=batch,
        ),
        name="cross_layer",
    )(me, rows, sel, scale, scale.T, bottom, labels, up, down, bias, ow)


def scatter_kernel(sel_ref, grad_ref, out_ref):
    out_ref[...] = jnp.dot(
        sel_ref[...], grad_ref[...], preferred_element_type=F32
    ).astype(out_ref.dtype)


def scatter_rows(sel, grad, dtype):
    tile = 512
    count, bags = sel.shape
    return pl.pallas_call(
        scatter_kernel,
        grid=(count // tile,),
        in_specs=[
            pl.BlockSpec((tile, bags), lambda i: (i, 0)),
            pl.BlockSpec((bags, EMB), lambda i: (0, 0)),
        ],
        out_specs=pl.BlockSpec((tile, EMB), lambda i: (i, 0)),
        out_shape=jax.ShapeDtypeStruct((count, EMB), dtype),
        cost_estimate=pl.CostEstimate(
            flops=2 * count * bags * EMB, bytes_accessed=count * bags * 2, transcendentals=0
        ),
        name="scatter_rows",
    )(sel, grad)


def serve_kernel(picks_ref, hot_picks_ref, count_ref, table_ref, out_ref):
    hot = []
    for s in range(hot_picks_ref.shape[0]):
        start = pl.multiple_of(hot_picks_ref[s] * BLOCK, BLOCK)
        rows = table_ref[pl.ds(start, BLOCK), :]
        hot.append(jnp.where(s < count_ref[0], rows, jnp.zeros_like(rows)))
    for i in range(out_ref.shape[0]):
        start = pl.multiple_of(picks_ref[i] * BLOCK, BLOCK)
        out_ref[i, :BLOCK, :] = table_ref[pl.ds(start, BLOCK), :]
        for s, rows in enumerate(hot):
            out_ref[i, (s + 1) * BLOCK : (s + 2) * BLOCK, :] = rows


def served_rows(emb_table, picks, hot_picks, count):
    smem = pl.BlockSpec(memory_space=pltpu.SMEM)
    vmem = pl.BlockSpec(memory_space=pltpu.VMEM)
    share = (1 + hot_picks.shape[0]) * BLOCK
    return pl.pallas_call(
        serve_kernel,
        in_specs=[smem, smem, smem, vmem],
        out_shape=jax.ShapeDtypeStruct((picks.shape[0], share, EMB), BF),
        name="served_rows",
    )(picks, hot_picks, count, emb_table)


def collect_kernel(picks_ref, hot_picks_ref, count_ref, me_ref, back_ref, own_ref, *others):
    *send_refs, acc = others
    acc[...] = jnp.zeros_like(acc)
    peers, share, _ = back_ref.shape
    hot = jnp.zeros((share - BLOCK, EMB), F32)
    for i in range(peers):
        start = pl.multiple_of(picks_ref[i] * BLOCK, BLOCK)
        acc[pl.ds(start, BLOCK), :] += back_ref[i, :BLOCK, :].astype(F32)
        hot = hot + back_ref[i, BLOCK:, :].astype(F32)
    for s in range(hot_picks_ref.shape[0]):
        start = pl.multiple_of(hot_picks_ref[s] * BLOCK, BLOCK)
        rows = hot[s * BLOCK : (s + 1) * BLOCK]
        acc[pl.ds(start, BLOCK), :] += jnp.where(s < count_ref[0], rows, jnp.zeros_like(rows))
    part, parts = own_ref.shape[0], len(send_refs) + 1
    for k, ref in enumerate((own_ref, *send_refs)):
        whose = lax.rem(me_ref[0] + k, parts)
        start = pl.multiple_of(whose * part, part)
        ref[...] = acc[pl.ds(start, part), :].astype(ref.dtype)


def collected(rows, parts, picks, hot_picks, count, me, back):
    smem = pl.BlockSpec(memory_space=pltpu.SMEM)
    vmem = pl.BlockSpec(memory_space=pltpu.VMEM)
    return pl.pallas_call(
        collect_kernel,
        in_specs=[smem, smem, smem, smem, vmem],
        out_shape=[
            jax.ShapeDtypeStruct((rows // parts, EMB), BF if k else F32) for k in range(parts)
        ],
        scratch_shapes=[pltpu.VMEM((rows, EMB), F32)],
        name="collected",
    )(picks, hot_picks, count, me, back)


def slots_kernel(cold, hot_slots, tries, ids_ref, weight_ref, length_ref, slots_ref, scale_ref):
    bag = ids_ref.shape[0]
    length = length_ref[...]
    row_bits = BLOCK.bit_length() - 1
    cold_bits = cold.bit_length() - 1
    ids, coef = [], []
    for s in range(bag):
        i = ids_ref[s]
        slot, rest = i >> cold_bits, i & (cold - 1)
        owner, row = rest >> row_bits, rest & (BLOCK - 1)
        ids.append((owner * (1 + hot_slots) + slot) * BLOCK + row)
        coef.append(jnp.where(s < length, weight_ref[s], 0.0))
    total = []
    for j in range(bag):
        c = coef[j]
        for i in range(j):
            c = c + jnp.where(ids[i] == ids[j], coef[i], 0.0)
        total.append(c)
    kept = []
    for j in range(bag):
        c = total[j]
        for k in range(j + 1, bag):
            c = jnp.where(ids[j] == ids[k], 0.0, c)
        kept.append(c)
    largest = functools.reduce(jnp.maximum, kept)
    inverse = 1.0 / largest

    def attempt(k, carry):
        best, scale, factor = carry
        t = 1.0 + k.astype(F32) * (1.0 / tries)
        up = inverse * t
        back = largest * (1.0 / t)
        err = jnp.zeros_like(largest)
        for c in kept:
            miss = (c * up).astype(BF).astype(F32) * back - c
            err = err + miss * miss
        better = err < best
        return (
            jnp.where(better, err, best),
            jnp.where(better, back, scale),
            jnp.where(better, up, factor),
        )

    start = (jnp.full_like(largest, jnp.inf), largest, inverse)
    _, scale, factor = lax.fori_loop(0, tries, attempt, start)
    for s in range(bag):
        slots_ref[s] = ids[s].astype(F32)
        slots_ref[bag + s] = kept[s] * factor
    scale_ref[...] = scale


def bag_slots(ids, weight, length, owners, hot_slots):
    cold = owners * BLOCK
    batch, feats, bag = ids.shape
    slots, scale = pl.pallas_call(
        functools.partial(slots_kernel, cold, hot_slots, 64),
        out_shape=[
            jax.ShapeDtypeStruct((2 * bag, feats, batch), F32),
            jax.ShapeDtypeStruct((feats, batch), F32),
        ],
        name="bag_slots",
    )(jnp.transpose(ids, (2, 1, 0)), jnp.transpose(weight, (2, 1, 0)), length.T)
    return jnp.transpose(slots, (1, 0, 2)), scale


def permuted(parts, axis):
    size = lax.axis_size(axis)
    return [
        lax.ppermute(part, axis, [(i, (i + k) % size) for i in range(size)])
        for k, part in enumerate(parts, 1)
    ]


def local(
    emb_table,
    cross_up,
    cross_down,
    cross_bias,
    out_weight,
    bottom_weight,
    bottom_bias,
    dense_in,
    labels,
    lookup_ids,
    bag_weight,
    bag_length,
    want_blocks,
    hot_blocks,
    hot_count,
):
    owners = lax.axis_size(TABLE)
    replicas = lax.axis_size("replica")
    hot_slots = hot_blocks.shape[1]
    _, width = cross_up.shape

    wanted = want_blocks.reshape(owners, 1, 1)
    asked_for = lax.all_to_all(wanted, TABLE, split_axis=0, concat_axis=0, tiled=True)
    asked_for = asked_for.reshape(owners)
    served = served_rows(emb_table, asked_for, hot_blocks[0], hot_count)
    fetched = lax.all_to_all(served, TABLE, split_axis=0, concat_axis=0, tiled=True)
    shares = fetched.shape
    fetched = fetched.reshape(-1, EMB)

    slots, scale = bag_slots(lookup_ids, bag_weight, bag_length, owners, hot_slots)
    sel = build_selection(slots, 0, fetched.shape[0])

    bottom = jax.nn.relu(
        jnp.dot(dense_in, bottom_weight, precision=lax.Precision.HIGHEST) + bottom_bias
    )
    me = lax.axis_index("replica").reshape(1)
    cores = lax.axis_size("table_2")
    xs = lax.axis_size("table_1")
    assert xs == XS
    grad_pooled, own, *sends = cross_layer(
        cores * replicas,
        replicas,
        me,
        fetched,
        sel,
        scale,
        bottom,
        labels[:, None],
        cross_up,
        cross_down,
        cross_bias[None],
        out_weight[None],
    )

    got = permuted(sends, "replica")

    row_grad = scatter_rows(sel, grad_pooled, BF).reshape(shares)
    returned = lax.all_to_all(row_grad, TABLE, split_axis=0, concat_axis=0, tiled=True)

    nearer = own
    for part in got:
        nearer = nearer + part.astype(F32)
    nearer = nearer.reshape(cores, xs, -1, EMB)
    x = lax.axis_index("table_1")
    turned = [
        lax.dynamic_index_in_dim(nearer, lax.rem(x + k, xs), 1, keepdims=False)
        for k in range(xs)
    ]
    got = permuted([part.astype(BF) for part in turned[1:]], "table_1")
    nearest = turned[0]
    for part in got:
        nearest = nearest + part.astype(F32)
    nearest = nearest.astype(BF)
    nearest, returned = lax.optimization_barrier((nearest, returned))

    own, *sends = collected(
        emb_table.shape[0], replicas, asked_for, hot_blocks[0], hot_count, me, returned
    )
    got = permuted(sends, "replica")
    table_grad = own
    for part in got:
        table_grad = table_grad + part.astype(F32)

    group = ("table_2", "table_0")
    mine = nearest.reshape(lax.axis_size(group), -1, EMB)
    mine = lax.all_to_all(mine, group, split_axis=0, concat_axis=0, tiled=True)
    per = 2 * width // EMB
    mine = mine.astype(F32).sum(axis=0)[:per].reshape(1, 2 * width)
    up_grad, down_grad = mine[:, :width], mine[:, width:]
    return (up_grad, down_grad, table_grad)


def solution(mesh):
    torus = Mesh(
        mesh.devices.reshape(8, 4, 2, mesh.shape["replica"]),
        ("table_0", "table_1", "table_2", "replica"),
    )
    in_specs = (
        P(TABLE, None),
        P(),
        P(),
        P(),
        P(),
        P(),
        P(),
        P(TABLE_REPLICA, None),
        P(TABLE_REPLICA),
        P(TABLE_REPLICA, None, None),
        P(TABLE_REPLICA, None, None),
        P(TABLE_REPLICA, None),
        P(TABLE, "replica", None, None),
        P(TABLE, None),
        P(TABLE),
    )
    out_specs = (P(TABLE_REPLICA, None), P(TABLE_REPLICA, None), P(TABLE_REPLICA, None))
    return jax.shard_map(local, mesh=torus, in_specs=in_specs, out_specs=out_specs, check_vma=False)
```

```python
import functools

import jax
import jax.numpy as jnp
from jax import lax
from jax.experimental import pallas as pl
from jax.experimental.pallas import tpu as pltpu
from jax.sharding import Mesh
from jax.sharding import PartitionSpec as P

EMB = 128
BLOCK = 32
TABLE = ("table_0", "table_1", "table_2")
TABLE_REPLICA = ("table_0", "table_1", "table_2", "replica")
BF = jnp.bfloat16
F32 = jnp.float32
XS = 4


def build_kernel(first, tile, slots_ref, out_ref):
    base = (first + pl.program_id(0) * tile).astype(F32)
    feats, _, batch = slots_ref.shape
    rows = lax.broadcasted_iota(jnp.int32, (tile, batch), 0).astype(F32).astype(BF)

    def one(f, carry):
        packed = slots_ref[f]
        rel = jnp.clip(packed[:4] - base, -1.0, float(tile)).astype(BF)
        coef = packed[4:].astype(BF)
        acc = jnp.zeros((tile, batch), BF)
        for s in range(4):
            hit = rows == jnp.broadcast_to(rel[s : s + 1], (tile, batch))
            acc = jnp.where(hit, jnp.broadcast_to(coef[s : s + 1], (tile, batch)), acc)
        out_ref[:, pl.ds(pl.multiple_of(f * batch, batch), batch)] = acc
        return carry

    lax.fori_loop(0, feats, one, 0)


def build_selection(slots, first, count):
    tile = 256
    feats, _, batch = slots.shape
    bags = feats * batch
    return pl.pallas_call(
        functools.partial(build_kernel, first, tile),
        grid=(count // tile,),
        in_specs=[
            pl.BlockSpec((feats, 8, batch), lambda i: (0, 0, 0)),
        ],
        out_specs=pl.BlockSpec((tile, bags), lambda i: (i, 0)),
        out_shape=jax.ShapeDtypeStruct((count, bags), BF),
        cost_estimate=pl.CostEstimate(
            flops=count * bags * 8, bytes_accessed=count * bags * 2, transcendentals=0
        ),
        name="build_selection",
    )(slots)


def build_hot_kernel(first, tile, me_ref, slots_ref, rows_ref, sel_ref, pooled_ref):
    build_kernel(first, tile, slots_ref, sel_ref)
    part = lax.dot_general(
        rows_ref[...], sel_ref[...], (((0,), (0,)), ((), ())), preferred_element_type=F32
    )

    @pl.when(pl.program_id(0) == 0)
    def _():
        pooled_ref[...] = part

    @pl.when(pl.program_id(0) > 0)
    def _():
        pooled_ref[...] += part


def build_hot(me, slots, pieces, first, replicas):
    tile = 256
    feats, _, batch = slots.shape
    bags = feats * batch
    count = pieces.shape[0]
    per = count // replicas // tile

    def rows_map(i, me):
        return lax.rem(me[0] - i // per + replicas, replicas) * per + i % per, 0

    return pl.pallas_call(
        functools.partial(build_hot_kernel, first, tile),
        grid_spec=pltpu.PrefetchScalarGridSpec(
            num_scalar_prefetch=1,
            grid=(count // tile,),
            in_specs=[
                pl.BlockSpec((feats, 8, batch), lambda i, me: (0, 0, 0)),
                pl.BlockSpec((tile, EMB), rows_map),
            ],
            out_specs=[
                pl.BlockSpec((tile, bags), lambda i, me: (i, 0)),
                pl.BlockSpec((EMB, bags), lambda i, me: (0, 0)),
            ],
        ),
        out_shape=[
            jax.ShapeDtypeStruct((count, bags), BF),
            jax.ShapeDtypeStruct((EMB, bags), F32),
        ],
        cost_estimate=pl.CostEstimate(
            flops=count * bags * 256, bytes_accessed=count * bags * 2, transcendentals=0
        ),
        name="build_hot",
    )(me, slots, pieces)


def cross_kernel(
    near,
    replicas,
    me_ref,
    rows_ref,
    sel_ref,
    hot_ref,
    scale_ref,
    scale_t_ref,
    bottom_ref,
    labels_ref,
    up_ref,
    down_ref,
    bias_ref,
    ow_ref,
    gpool_ref,
    own_ref,
    *others,
):
    *send_refs, acc, base_ref, lines_ref = others
    step = pl.program_id(0)
    part = lax.dot_general(
        rows_ref[...], sel_ref[...], (((0,), (0,)), ((), ())), preferred_element_type=F32
    )

    @pl.when(step == 0)
    def _():
        acc[...] = hot_ref[...] + part

    @pl.when(step > 0)
    def _():
        acc[...] += part

    @pl.when(step == pl.num_programs(0) - 1)
    def _():
        batch = bottom_ref.shape[0]
        width = up_ref.shape[1]
        feats = width // EMB - 1
        base_ref[:, :EMB] = bottom_ref[...].astype(BF)
        for f in range(feats):
            block = acc[:, f * batch : (f + 1) * batch]
            base_ref[:, (f + 1) * EMB : (f + 2) * EMB] = (block * scale_ref[f : f + 1, :]).T.astype(BF)
        base = base_ref[...]
        nt = (((1,), (1,)), ((), ()))
        tn = (((0,), (0,)), ((), ()))
        low = lax.dot_general(base, down_ref[...], nt, preferred_element_type=F32).astype(BF)
        wide = base.astype(F32)
        ow = ow_ref[...]
        gate = jnp.dot(low, up_ref[...], preferred_element_type=F32) + bias_ref[...]
        crossed = wide * gate + wide
        logits = jnp.sum(crossed * ow, axis=1, keepdims=True)
        lg = jax.nn.sigmoid(logits) - labels_ref[...].astype(F32)
        grad_crossed = lg * ow
        g_cross = (grad_crossed * wide).astype(BF)
        g_low = lax.dot_general(g_cross, up_ref[...], nt, preferred_element_type=F32).astype(BF)
        up_part = lax.dot_general(low, g_cross, tn, preferred_element_type=F32)
        down_part = lax.dot_general(g_low, base, tn, preferred_element_type=F32)
        rank, per = up_part.shape[0], feats + 1
        lines = lines_ref.shape[0] // rank
        far = rank // near
        for z in range(far):
            part_rows = slice(z * near, (z + 1) * near)
            for c in range(lines):
                if c < per:
                    part = up_part[part_rows, c * EMB : (c + 1) * EMB]
                elif c < 2 * per:
                    part = down_part[part_rows, (c - per) * EMB : (c - per + 1) * EMB]
                else:
                    part = jnp.zeros((near, EMB), F32)
                place = (z % XS) * (far // XS) + z // XS
                lines_ref[pl.ds(place * lines + c, near, stride=far * lines), :] = part
        for k, ref in enumerate((own_ref, *send_refs)):
            whose = lax.rem(me_ref[0] + k, replicas)
            for core in range(near // replicas):
                start = pl.multiple_of((core * replicas + whose) * far * lines, far * lines)
                ref[core] = lines_ref[pl.ds(start, far * lines), :].astype(ref.dtype)
        grad_base = grad_crossed * (gate + 1.0) + jnp.dot(
            g_low, down_ref[...], preferred_element_type=F32
        )
        for f in range(feats):
            block = grad_base[:, (f + 1) * EMB : (f + 2) * EMB] * scale_t_ref[:, f : f + 1]
            gpool_ref[f * batch : (f + 1) * batch, :] = block.astype(BF)


def cross_layer(near, replicas, me, rows, sel, hot, scale, bottom, labels, up, down, bias, ow):
    tile = 512
    count, bags = sel.shape
    rank, width = up.shape
    batch = bottom.shape[0]
    lines = rank * pl.cdiv(2 * width // EMB, 8) * 8
    part = (near // replicas, lines // near, EMB)
    whole = lambda *shape: pl.BlockSpec(shape, lambda i: (0,) * len(shape))
    return pl.pallas_call(
        functools.partial(cross_kernel, near, replicas),
        grid=(count // tile,),
        in_specs=[
            pl.BlockSpec(memory_space=pltpu.SMEM),
            pl.BlockSpec((tile, EMB), lambda i: (i, 0)),
            pl.BlockSpec((tile, bags), lambda i: (i, 0)),
            whole(EMB, bags),
            whole(*scale.shape),
            whole(batch, scale.shape[0]),
            whole(batch, EMB),
            whole(batch, 1),
            whole(rank, width),
            whole(rank, width),
            whole(1, width),
            whole(1, width),
        ],
        out_specs=[whole(bags, EMB)] + [whole(*part)] * replicas,
        out_shape=[
            jax.ShapeDtypeStruct((bags, EMB), BF),
            *(jax.ShapeDtypeStruct(part, BF if k else F32) for k in range(replicas)),
        ],
        scratch_shapes=[
            pltpu.VMEM((EMB, bags), F32),
            pltpu.VMEM((batch, width), BF),
            pltpu.VMEM((lines, EMB), F32),
        ],
        cost_estimate=pl.CostEstimate(
            flops=2 * count * bags * EMB + 12 * batch * rank * width,
            bytes_accessed=count * bags * 2 + 8 * rank * width,
            transcendentals=batch,
        ),
        name="cross_layer",
    )(me, rows, sel, hot, scale, scale.T, bottom, labels, up, down, bias, ow)


def scatter_kernel(cold_ref, hot_ref, grad_ref, out_ref):
    grad = grad_ref[...]
    some = out_ref.shape[0]
    cold = jnp.dot(cold_ref[...], grad, preferred_element_type=F32).astype(BF)
    out_ref[:, :BLOCK, :] = cold.reshape(some, BLOCK, EMB)
    for piece in range(hot_ref.shape[0]):
        part = jnp.dot(hot_ref[piece], grad, preferred_element_type=F32).astype(BF)
        share = part.shape[0] // some
        start = BLOCK + piece * share
        out_ref[:, start : start + share, :] = part.reshape(some, share, EMB)


def scatter_rows(cold, hot, grad, owners, pieces):
    some = 8
    bags = cold.shape[1]
    share = hot.shape[0] // (owners * pieces)
    each = BLOCK + pieces * share
    return pl.pallas_call(
        scatter_kernel,
        grid=(owners // some,),
        in_specs=[
            pl.BlockSpec((some * BLOCK, bags), lambda i: (i, 0)),
            pl.BlockSpec((pieces, some * share, bags), lambda i: (0, i, 0)),
            pl.BlockSpec((bags, EMB), lambda i: (0, 0)),
        ],
        out_specs=pl.BlockSpec((some, each, EMB), lambda i: (i, 0, 0)),
        out_shape=jax.ShapeDtypeStruct((owners, each, EMB), BF),
        cost_estimate=pl.CostEstimate(
            flops=2 * owners * each * bags * EMB,
            bytes_accessed=owners * each * bags * 2,
            transcendentals=0,
        ),
        name="scatter_rows",
    )(cold, hot.reshape(pieces, owners * share, bags), grad)


def hot_kernel(picks_ref, count_ref, me_ref, table_ref, out_ref):
    peers, share, _ = out_ref.shape
    shares = BLOCK // share
    slot, part = lax.div(me_ref[0], shares), lax.rem(me_ref[0], shares)
    start = pl.multiple_of(picks_ref[slot] * BLOCK + part * share, share)
    rows = table_ref[pl.ds(start, share), :]
    rows = jnp.where(slot < count_ref[0], rows, jnp.zeros_like(rows))
    for i in range(peers):
        out_ref[i] = rows


def hot_share(emb_table, peers, share, picks, count, me):
    smem = pl.BlockSpec(memory_space=pltpu.SMEM)
    vmem = pl.BlockSpec(memory_space=pltpu.VMEM)
    return pl.pallas_call(
        hot_kernel,
        in_specs=[smem, smem, smem, vmem],
        out_shape=jax.ShapeDtypeStruct((peers, share, EMB), BF),
        name="hot_share",
    )(picks, count, me, emb_table)


def serve_kernel(picks_ref, table_ref, out_ref):
    for i in range(out_ref.shape[0]):
        start = pl.multiple_of(picks_ref[i] * BLOCK, BLOCK)
        out_ref[i] = table_ref[pl.ds(start, BLOCK), :]


def served_rows(emb_table, picks):
    smem = pl.BlockSpec(memory_space=pltpu.SMEM)
    vmem = pl.BlockSpec(memory_space=pltpu.VMEM)
    return pl.pallas_call(
        serve_kernel,
        in_specs=[smem, vmem],
        out_shape=jax.ShapeDtypeStruct((picks.shape[0], BLOCK, EMB), BF),
        name="served_rows",
    )(picks, emb_table)


def collect_kernel(picks_ref, hot_picks_ref, count_ref, me_ref, back_ref, own_ref, *others):
    *send_refs, acc = others
    acc[...] = jnp.zeros_like(acc)
    peers, share, _ = back_ref.shape
    hot = jnp.zeros((share - BLOCK, EMB), F32)
    for i in range(peers):
        start = pl.multiple_of(picks_ref[i] * BLOCK, BLOCK)
        acc[pl.ds(start, BLOCK), :] += back_ref[i, :BLOCK, :].astype(F32)
        hot = hot + back_ref[i, BLOCK:, :].astype(F32)
    for s in range(hot_picks_ref.shape[0]):
        start = pl.multiple_of(hot_picks_ref[s] * BLOCK, BLOCK)
        rows = hot[s * BLOCK : (s + 1) * BLOCK]
        acc[pl.ds(start, BLOCK), :] += jnp.where(s < count_ref[0], rows, jnp.zeros_like(rows))
    part, parts = own_ref.shape[0], len(send_refs) + 1
    for k, ref in enumerate((own_ref, *send_refs)):
        whose = lax.rem(me_ref[0] + k, parts)
        start = pl.multiple_of(whose * part, part)
        ref[...] = acc[pl.ds(start, part), :].astype(ref.dtype)


def collected(rows, parts, picks, hot_picks, count, me, back):
    smem = pl.BlockSpec(memory_space=pltpu.SMEM)
    vmem = pl.BlockSpec(memory_space=pltpu.VMEM)
    return pl.pallas_call(
        collect_kernel,
        in_specs=[smem, smem, smem, smem, vmem],
        out_shape=[
            jax.ShapeDtypeStruct((rows // parts, EMB), BF if k else F32) for k in range(parts)
        ],
        scratch_shapes=[pltpu.VMEM((rows, EMB), F32)],
        name="collected",
    )(picks, hot_picks, count, me, back)


def slots_kernel(cold, share, tries, ids_ref, weight_ref, length_ref, slots_ref, scale_ref):
    bag = ids_ref.shape[0]
    length = length_ref[...]
    row_bits = BLOCK.bit_length() - 1
    cold_bits = cold.bit_length() - 1
    share_bits = share.bit_length() - 1
    ids, coef = [], []
    for s in range(bag):
        i = ids_ref[s]
        h = i - cold
        slot, rest = h >> cold_bits, h & (cold - 1)
        owner, row = rest >> row_bits, (slot << row_bits) + (rest & (BLOCK - 1))
        piece, row = row >> share_bits, row & (share - 1)
        moved = cold + piece * (cold // BLOCK * share) + owner * share + row
        ids.append(jnp.where(i < cold, i, moved))
        coef.append(jnp.where(s < length, weight_ref[s], 0.0))
    total = []
    for j in range(bag):
        c = coef[j]
        for i in range(j):
            c = c + jnp.where(ids[i] == ids[j], coef[i], 0.0)
        total.append(c)
    kept = []
    for j in range(bag):
        c = total[j]
        for k in range(j + 1, bag):
            c = jnp.where(ids[j] == ids[k], 0.0, c)
        kept.append(c)
    largest = functools.reduce(jnp.maximum, kept)
    inverse = 1.0 / largest

    def attempt(k, carry):
        best, scale, factor = carry
        t = 1.0 + k.astype(F32) * (1.0 / tries)
        up = inverse * t
        back = largest * (1.0 / t)
        err = jnp.zeros_like(largest)
        for c in kept:
            miss = (c * up).astype(BF).astype(F32) * back - c
            err = err + miss * miss
        better = err < best
        return (
            jnp.where(better, err, best),
            jnp.where(better, back, scale),
            jnp.where(better, up, factor),
        )

    start = (jnp.full_like(largest, jnp.inf), largest, inverse)
    _, scale, factor = lax.fori_loop(0, tries, attempt, start)
    for s in range(bag):
        slots_ref[s] = ids[s].astype(F32)
        slots_ref[bag + s] = kept[s] * factor
    scale_ref[...] = scale


def bag_slots(ids, weight, length, owners, share):
    cold = owners * BLOCK
    batch, feats, bag = ids.shape
    slots, scale = pl.pallas_call(
        functools.partial(slots_kernel, cold, share, 64),
        out_shape=[
            jax.ShapeDtypeStruct((2 * bag, feats, batch), F32),
            jax.ShapeDtypeStruct((feats, batch), F32),
        ],
        name="bag_slots",
    )(jnp.transpose(ids, (2, 1, 0)), jnp.transpose(weight, (2, 1, 0)), length.T)
    return jnp.transpose(slots, (1, 0, 2)), scale


def permuted(parts, axis):
    size = lax.axis_size(axis)
    return [
        lax.ppermute(part, axis, [(i, (i + k) % size) for i in range(size)])
        for k, part in enumerate(parts, 1)
    ]


def local(
    emb_table,
    cross_up,
    cross_down,
    cross_bias,
    out_weight,
    bottom_weight,
    bottom_bias,
    dense_in,
    labels,
    lookup_ids,
    bag_weight,
    bag_length,
    want_blocks,
    hot_blocks,
    hot_count,
):
    owners = lax.axis_size(TABLE)
    replicas = lax.axis_size("replica")
    hot_slots = hot_blocks.shape[1]
    _, width = cross_up.shape

    me = lax.axis_index("replica").reshape(1)
    share = hot_slots * BLOCK // replicas
    own_hot = hot_share(emb_table, owners, share, hot_blocks[0], hot_count, me)
    piece = lax.all_to_all(own_hot, TABLE, split_axis=0, concat_axis=0, tiled=True)
    piece = piece.reshape(-1, EMB)
    pieces = jnp.concatenate([piece, *permuted([piece] * (replicas - 1), "replica")], 0)

    wanted, piece = lax.optimization_barrier((want_blocks.reshape(owners, 1, 1), piece))
    asked_for = lax.all_to_all(wanted, TABLE, split_axis=0, concat_axis=0, tiled=True)
    asked_for = asked_for.reshape(owners)
    served = served_rows(emb_table, asked_for)
    fetched = lax.all_to_all(served, TABLE, split_axis=0, concat_axis=0, tiled=True)
    fetched = fetched.reshape(-1, EMB)

    slots, scale = bag_slots(lookup_ids, bag_weight, bag_length, owners, share)
    sel = build_selection(slots, 0, fetched.shape[0])
    sel_hot, pooled_hot = build_hot(me, slots, pieces, fetched.shape[0], replicas)

    bottom = jax.nn.relu(
        jnp.dot(dense_in, bottom_weight, precision=lax.Precision.HIGHEST) + bottom_bias
    )
    cores = lax.axis_size("table_2")
    xs = lax.axis_size("table_1")
    assert xs == XS
    grad_pooled, own, *sends = cross_layer(
        cores * replicas,
        replicas,
        me,
        fetched,
        sel,
        pooled_hot,
        scale,
        bottom,
        labels[:, None],
        cross_up,
        cross_down,
        cross_bias[None],
        out_weight[None],
    )

    got = permuted(sends, "replica")

    row_grad = scatter_rows(sel, sel_hot, grad_pooled, owners, replicas)
    returned = lax.all_to_all(row_grad, TABLE, split_axis=0, concat_axis=0, tiled=True)

    nearer = own
    for part in got:
        nearer = nearer + part.astype(F32)
    nearer = nearer.reshape(cores, xs, -1, EMB)
    x = lax.axis_index("table_1")
    turned = [
        lax.dynamic_index_in_dim(nearer, lax.rem(x + k, xs), 1, keepdims=False)
        for k in range(xs)
    ]
    got = permuted([part.astype(BF) for part in turned[1:]], "table_1")
    nearest = turned[0]
    for part in got:
        nearest = nearest + part.astype(F32)
    nearest = nearest.astype(BF)
    nearest, returned = lax.optimization_barrier((nearest, returned))

    own, *sends = collected(
        emb_table.shape[0], replicas, asked_for, hot_blocks[0], hot_count, me, returned
    )
    got = permuted(sends, "replica")
    table_grad = own
    for part in got:
        table_grad = table_grad + part.astype(F32)

    group = ("table_2", "table_0")
    mine = nearest.reshape(lax.axis_size(group), -1, EMB)
    mine = lax.all_to_all(mine, group, split_axis=0, concat_axis=0, tiled=True)
    per = 2 * width // EMB
    mine = mine.astype(F32).sum(axis=0)[:per].reshape(1, 2 * width)
    up_grad, down_grad = mine[:, :width], mine[:, width:]
    return (up_grad, down_grad, table_grad)


def solution(mesh):
    torus = Mesh(
        mesh.devices.reshape(8, 4, 2, mesh.shape["replica"]),
        ("table_0", "table_1", "table_2", "replica"),
    )
    in_specs = (
        P(TABLE, None),
        P(),
        P(),
        P(),
        P(),
        P(),
        P(),
        P(TABLE_REPLICA, None),
        P(TABLE_REPLICA),
        P(TABLE_REPLICA, None, None),
        P(TABLE_REPLICA, None, None),
        P(TABLE_REPLICA, None),
        P(TABLE, "replica", None, None),
        P(TABLE, None),
        P(TABLE),
    )
    out_specs = (P(TABLE_REPLICA, None), P(TABLE_REPLICA, None), P(TABLE_REPLICA, None))
    return jax.shard_map(local, mesh=torus, in_specs=in_specs, out_specs=out_specs, check_vma=False)
```
